512 devices in a mesh: aisle: 32 (over z_hi, y), span: 16 (over x, z_lo, core).
Axes of the slice: x: 4, y: 8, z: 8 (z_hi: 4, z_lo: 2; z = z_hi * 2 + z_lo), core: 2. Of those that a mesh axis runs over, the one named last changes fastest.
Arguments:
- downflow_motion: float32 [512, 512, 256], P('aisle', 'span'), may hold values from -6 to 6
- crossflow_motion: float32 [512, 512, 256], P('aisle', 'span'), may hold values from -6 to 6
- upright_motion: float32 [512, 512, 256], P('aisle', 'span'), may hold values from -6 to 6
- thermal_anomaly: float32 [512, 512, 256], P('aisle', 'span'), may hold values from -6 to 6
- height_to_eigenbasis: float32 [256, 256], replicated, may hold values from -1 to 2
- eigenbasis_to_height: float32 [256, 256], replicated, may hold values from -1 to 2
- negated_height_spectrum: float32 [256], replicated, may hold values from 0.002 to 0.02
Outputs:
- east_after: float32 [512, 512, 256], P('aisle', 'span')
- north_after: float32 [512, 512, 256], P('aisle', 'span')
- upward_after: float32 [512, 512, 256], P('aisle', 'span')
- heat_after: float32 [512, 512, 256], P('aisle', 'span')
The draws below stay inside these ranges and needn't reach their ends.
All inputs are finite; a program needn't handle non-finite values.
Results may differ from the reference program's by a relative error of at most 0.0003.
Values sent between devices are 32-bit elements; how exact they have to be, the bound alone decides.
No kernel may reach another device: no remote copies, remote signals or barrier semaphores. Data moves between devices by JAX's collectives and lax.ppermute only.
A program may use at most 128 MiB of HBM per device.

```python
import math
import jax
import jax.numpy as jnp
from jax import lax

DOWNFLOW_POINTS = 512
CROSSFLOW_POINTS = 512
GAP_POINTS = 256


def wind_field(key, salt):
    inner = jax.random.fold_in(key, salt)
    shape = (DOWNFLOW_POINTS, CROSSFLOW_POINTS, GAP_POINTS)
    return jax.random.truncated_normal(inner, -6.0, 6.0, shape, jnp.float32)


def draw_downflow_motion(key, part):
    return wind_field(key, 31)


def draw_crossflow_motion(key, part):
    return wind_field(key, 37)


def draw_height_to_eigenbasis(key, part):
    inner = jax.random.fold_in(key, 11)
    noise = jax.random.truncated_normal(inner, -4.0, 4.0, (GAP_POINTS, GAP_POINTS), jnp.float32)
    return jnp.eye(GAP_POINTS, dtype=jnp.float32) + 0.35 / math.sqrt(GAP_POINTS) * noise


def draw_eigenbasis_to_height(key, part):
    inner = jax.random.fold_in(key, 23)
    noise = jax.random.truncated_normal(inner, -4.0, 4.0, (GAP_POINTS, GAP_POINTS), jnp.float32)
    return jnp.eye(GAP_POINTS, dtype=jnp.float32) + 0.35 / math.sqrt(GAP_POINTS) * noise


def levels(key, dims, cuts, least, top_value):
    loudness = 1.0
    for position, shards_of in cuts:
        draws = jax.random.uniform(jax.random.fold_in(jax.random.fold_in(key, 6), position), (shards_of,), jnp.float32, least / len(cuts), top_value / len(cuts))
        loudness = loudness * jnp.repeat(jnp.exp(draws), dims[position] // shards_of).reshape((-1,) + (1,) * (len(dims) - 1 - position))
    return loudness


def gaussian(key, shape, spread, limit, shards=(), kind=jnp.bfloat16):
    drawn = jax.random.normal(key, shape, jnp.float32) * spread
    if len(shards) > 0:
        drawn = levels(key, shape, shards, -0.22, 0.18) * drawn
    return jnp.clip(drawn, min=-limit, max=limit).astype(kind)


def setup_inputs(seed: int = 0) -> dict:
    key_list = jax.random.split(jax.random.key(seed), 8)
    return {
        "downflow_motion": draw_downflow_motion(jax.random.fold_in(key_list[7], 71), 0),
        "crossflow_motion": draw_crossflow_motion(jax.random.fold_in(key_list[7], 71), 0),
        "upright_motion": gaussian(key_list[2], (DOWNFLOW_POINTS, CROSSFLOW_POINTS, GAP_POINTS), 1.0, 6.0, ((0, 32), (1, 16)), jnp.float32),
        "thermal_anomaly": gaussian(key_list[3], (DOWNFLOW_POINTS, CROSSFLOW_POINTS, GAP_POINTS), 1.0, 6.0, ((0, 32), (1, 16)), jnp.float32),
        "height_to_eigenbasis": draw_height_to_eigenbasis(jax.random.fold_in(key_list[7], 71), 0),
        "eigenbasis_to_height": draw_eigenbasis_to_height(jax.random.fold_in(key_list[7], 71), 0),
        "negated_height_spectrum": jnp.clip(jnp.exp(jax.random.uniform(key_list[6], (GAP_POINTS,), jnp.float32, math.log(0.002), math.log(0.02))), 0.002, 0.02),
    }


step_gain = 0.1 * 8.0 / 15.0
viscosity = 0.01
smagorinsky = 0.05
prandtl = 0.7
buoyancy = 1.0
strain_floor = 0.25
highest = lax.Precision.HIGHEST

def predictor(padded):
    centre = padded[:, 1:-1, 1:-1, 1:-1]
    east_side = padded[:, 2:, 1:-1, 1:-1]
    west_side = padded[:, :-2, 1:-1, 1:-1]
    north_side = padded[:, 1:-1, 2:, 1:-1]
    south_side = padded[:, 1:-1, :-2, 1:-1]
    upper_side = padded[:, 1:-1, 1:-1, 2:]
    lower_side = padded[:, 1:-1, 1:-1, :-2]
    slope_east = 0.5 * (east_side - west_side)
    slope_north = 0.5 * (north_side - south_side)
    slope_upward = 0.5 * (upper_side - lower_side)
    laplace = east_side + west_side + (north_side + south_side) + (upper_side + lower_side) - 6.0 * centre
    strain = lax.optimization_barrier(jnp.sum(slope_east[:3] * slope_east[:3] + slope_north[:3] * slope_north[:3] + slope_upward[:3] * slope_upward[:3], axis=0))
    turbulent = viscosity + smagorinsky * jnp.sqrt(strain + strain_floor)
    transport = centre[0] * slope_east + centre[1] * slope_north + centre[2] * slope_upward
    diffusive = jnp.stack([turbulent, turbulent, turbulent, turbulent / prandtl])
    tendency = diffusive * laplace - transport
    tendency = jnp.concatenate([tendency[:2], tendency[2:3] + buoyancy * centre[3:4], tendency[3:]], axis=0)
    return centre + step_gain * tendency

def reference(downflow_motion, crossflow_motion, upright_motion, thermal_anomaly, height_to_eigenbasis, eigenbasis_to_height, negated_height_spectrum):
    bundled_unknowns = jnp.stack([downflow_motion, crossflow_motion, upright_motion, thermal_anomaly])
    padded = jnp.pad(bundled_unknowns, ((0, 0), (1, 1), (1, 1), (0, 0)), mode='wrap')
    padded = jnp.pad(padded, ((0, 0), (0, 0), (0, 0), (1, 1)))
    slab_size = math.gcd(DOWNFLOW_POINTS, 16)

    def one_slab(start):
        block = lax.dynamic_slice_in_dim(padded, start * slab_size, slab_size + 2, axis=1)
        return predictor(block)
    pieces = lax.map(one_slab, jnp.arange(DOWNFLOW_POINTS // slab_size, dtype=jnp.int32))
    predicted = jnp.moveaxis(pieces, 0, 1).reshape(4, DOWNFLOW_POINTS, CROSSFLOW_POINTS, GAP_POINTS)
    east_star = predicted[0]
    north_star = predicted[1]
    upward_star = predicted[2]
    heat_star = predicted[3]
    below = jnp.pad(upward_star[:, :, :-1], ((0, 0), (0, 0), (1, 0)))
    source = (east_star - jnp.roll(east_star, 1, axis=0) + (north_star - jnp.roll(north_star, 1, axis=1)) + (upward_star - below)) / step_gain
    vertical_modes = jnp.einsum('xyz,kz->xyk', source, height_to_eigenbasis, precision=highest)
    spectrum = jnp.fft.fft2(vertical_modes, axes=(0, 1))
    wave_x = jnp.sin(jnp.pi * jnp.arange(DOWNFLOW_POINTS, dtype=jnp.float32) / DOWNFLOW_POINTS)
    wave_y = jnp.sin(jnp.pi * jnp.arange(CROSSFLOW_POINTS, dtype=jnp.float32) / CROSSFLOW_POINTS)
    divisor = (-4.0 * wave_x * wave_x)[:, None, None] + (-4.0 * wave_y * wave_y)[None, :, None] - negated_height_spectrum[None, None, :]
    solved = jnp.real(jnp.fft.ifft2(spectrum / divisor, axes=(0, 1))).astype(downflow_motion.dtype)
    pressure = jnp.einsum('xyk,zk->xyz', solved, eigenbasis_to_height, precision=highest)
    above = jnp.pad(pressure[:, :, 1:], ((0, 0), (0, 0), (0, 1)))
    east_after = east_star - step_gain * (jnp.roll(pressure, -1, axis=0) - pressure)
    north_after = north_star - step_gain * (jnp.roll(pressure, -1, axis=1) - pressure)
    upward_after = upward_star - step_gain * (above - pressure)
    return (east_after, north_after, upward_after, heat_star)
```

```python
import functools
import math

import jax
import jax.numpy as jnp
import ml_dtypes
import numpy as np
from jax import lax
from jax.experimental import pallas as pl
from jax.experimental.pallas import tpu as pltpu
from jax.sharding import PartitionSpec as P

f32 = jnp.float32
bf16 = jnp.bfloat16
step_gain = 0.1 * 8.0 / 15.0
viscosity = 0.01
smagorinsky = 0.05
prandtl = 0.7
buoyancy = 1.0
strain_floor = 0.25

AISLE = 32
SPAN = 16
BX = 16
BY = 32
NZ = 256
NY = SPAN * BY
KS = NZ // SPAN
HALF = NY // 2
XR = BX + 1
ROWS = 72


def y_tables():
    cells = np.arange(HALF)
    even = [(m, 0) for m in range(0, HALF + 1, 2)] + [(m, 1) for m in range(2, HALF, 2)]
    odd = [(m, 0) for m in range(1, HALF, 2)] + [(m, 1) for m in range(1, HALF, 2)]
    modes = even + odd
    edges = (BY * (np.arange(SPAN) + 1)) % NY

    def rows(at):
        wave = np.array([m for m, _ in modes])
        odd_part = np.array([s for _, s in modes])
        angle = 2.0 * np.pi / NY * ((at[:, None] * wave[None, :]) % NY)
        return np.where(odd_part[None, :] == 1, np.sin(angle), np.cos(angle))

    main = rows(cells)
    extra = np.zeros((128, NY))
    extra[32 : 32 + SPAN] = rows(edges)
    table = np.concatenate([main, extra], axis=0).astype(np.float32)
    high = table.astype(ml_dtypes.bfloat16)
    low = (table - high.astype(np.float32)).astype(ml_dtypes.bfloat16)
    wave = np.array([m for m, _ in modes])
    eigen = (4.0 * np.sin(np.pi * wave / NY) ** 2).astype(np.float32)
    weight = np.where((wave == 0) | (wave == HALF), 1.0 / NY, 2.0 / NY).astype(np.float32)
    return high, low, eigen, weight


TABLE_HIGH, TABLE_LOW, EIGEN, WEIGHT = y_tables()


def split(value):
    high = value.astype(bf16)
    low = (value - high.astype(f32)).astype(bf16)
    return high, low


def dot3(a, b, dims):
    def one(p, q):
        return lax.dot_general(p, q, (dims, ((), ())), preferred_element_type=f32)

    return one(a[0], b[0]) + (one(a[0], b[1]) + one(a[1], b[0]))


NN = ((1,), (0,))
NT = ((1,), (1,))


def exchange(vectors, unit, lane):
    vectors = list(vectors)
    distance = len(vectors) // 2
    while distance:
        upper = (lane // (unit * distance)) % 2 == 1
        for i in range(len(vectors)):
            if i & distance:
                continue
            a, b = vectors[i], vectors[i + distance]
            vectors[i] = jnp.where(upper, pltpu.roll(b, unit * distance, 1), a)
            vectors[i + distance] = jnp.where(upper, b, pltpu.roll(a, 128 - unit * distance, 1))
        distance //= 2
    return vectors


def pack_kernel(*refs):
    x_first, x_last, y_first, y_last = refs[16:]
    for f in range(4):
        x_first[f] = refs[f][0]
        x_last[f] = refs[4 + f][0]
        y_first[f] = refs[8 + f][:, 0, :]
        y_last[f] = refs[12 + f][:, 7, :]


def pack(fields):
    plane = lambda at: pl.BlockSpec((1, BY, NZ), lambda i: (at, 0, 0))
    rows = lambda at: pl.BlockSpec((BX, 8, NZ), lambda i: (0, at, 0))
    whole = lambda shape: pl.BlockSpec(shape, lambda i: (0, 0, 0))
    xs, ys = (4, BY, NZ), (4, BX, NZ)
    return pl.pallas_call(
        pack_kernel,
        grid=(1,),
        in_specs=[plane(0)] * 4 + [plane(BX - 1)] * 4 + [rows(0)] * 4 + [rows(BY // 8 - 1)] * 4,
        out_specs=[whole(xs), whole(xs), whole(ys), whole(ys)],
        out_shape=[jax.ShapeDtypeStruct(s, f32) for s in (xs, xs, ys, ys)],
        name="pack",
    )(*fields, *fields, *fields, *fields)


def predict_kernel(
    fd, fc, fu, ft, xlo, xhi, ylo, yhi, basis, es, ns, us, ts, chunk, buf, src, sems
):
    copies = [pltpu.make_async_copy(f, buf.at[i, pl.ds(1, BX)], sems.at[i]) for i, f in enumerate((fd, fc, fu, ft))]
    copies.append(pltpu.make_async_copy(xlo, buf.at[:, 0], sems.at[4]))
    copies.append(pltpu.make_async_copy(xhi, buf.at[:, BX + 1], sems.at[5]))
    for copy in copies:
        copy.start()
    row = lax.broadcasted_iota(jnp.int32, (BY, NZ), 0)
    lane = lax.broadcasted_iota(jnp.int32, (BY, NZ), 1)
    base = BX * BY
    src[base + BY :, :] = jnp.zeros((128 - BY, NZ), f32)
    for copy in copies:
        copy.wait()
    zero = jnp.zeros((BY, NZ), f32)

    def south_of(value, edge):
        return jnp.where(row == 0, edge, pltpu.roll(value, 1, 0))

    def lower_of(value):
        return jnp.where(lane == 0, 0.0, pltpu.roll(value, 1, 1))

    def plane(x, east_prev):
        centre, steps, laplace = [], [], []
        for f in range(4):
            c = buf[f, x + 1]
            w, e = buf[f, x], buf[f, x + 2]
            s = south_of(c, ylo[f, pl.ds(x, 1), :])
            n = jnp.where(row == BY - 1, yhi[f, pl.ds(x, 1), :], pltpu.roll(c, BY - 1, 0))
            l = lower_of(c)
            u = jnp.where(lane == NZ - 1, 0.0, pltpu.roll(c, NZ - 1, 1))
            centre.append(c)
            steps.append((e - w, n - s, u - l))
            laplace.append((e + w) + (n + s) + (u + l) - 6.0 * c)
        strain = sum(d * d for f in range(3) for d in steps[f])
        turbulent = viscosity + smagorinsky * jnp.sqrt(0.25 * strain + strain_floor)
        stars = []
        for f in range(4):
            k = turbulent if f < 3 else turbulent * (1.0 / prandtl)
            dx, dy, dz = steps[f]
            transport = 0.5 * (centre[0] * dx + centre[1] * dy + centre[2] * dz)
            tendency = k * laplace[f] - transport
            if f == 2:
                tendency = tendency + buoyancy * centre[3]
            stars.append(centre[f] + step_gain * tendency)
        east, north, upward, heat = stars
        es[x] = east
        ns[x] = north
        us[x] = upward
        ts[x] = heat
        flux = (east - east_prev) + (north - south_of(north, zero)) + (upward - lower_of(upward))
        src[pl.ds(pl.multiple_of(x * BY, BY), BY), :] = flux
        src[pl.ds(base + BY + x, 1), :] = -north[BY - 1 :, :]
        return east

    last = lax.fori_loop(0, BX, plane, zero)
    src[base : base + BY, :] = -last
    forward = split(basis[...])
    for t in range(5):
        modes = dot3(forward, split(src[t * 128 : (t + 1) * 128, :]), NT)
        if t < 4:
            chunk[:, t * KS : (t + 1) * KS, :] = modes.reshape(SPAN, KS, 128)
        else:
            modes = modes.reshape(SPAN, 2, 8, 128)
            lanes = lax.broadcasted_iota(jnp.int32, (8, 128), 1)
            for s in range(SPAN):
                chunk[s, 4 * KS :, :] = jnp.where(lanes < 64, modes[s, 0], pltpu.roll(modes[s, 1], 64, 1))


def predict(fields, xlo, xhi, ylo, yhi, basis):
    any_spec = pl.BlockSpec(memory_space=pl.ANY)
    vmem = pl.BlockSpec(memory_space=pltpu.VMEM)
    block = jax.ShapeDtypeStruct((BX, BY, NZ), f32)
    return pl.pallas_call(
        predict_kernel,
        in_specs=[any_spec] * 6 + [vmem] * 3,
        out_specs=[vmem] * 5,
        out_shape=[block] * 4 + [jax.ShapeDtypeStruct((SPAN, ROWS, 128), f32)],
        scratch_shapes=[
            pltpu.VMEM((4, BX + 2, BY, NZ), f32),
            pltpu.VMEM((BX * BY + 128, NZ), f32),
            pltpu.SemaphoreType.DMA((6,)),
        ],
        name="predict",
    )(*fields, xlo, xhi, ylo, yhi, basis)


def decay(mu):
    root = jnp.sqrt(mu + 0.25 * mu * mu)
    return root, 1.0 / (1.0 + 0.5 * mu + root)


def transform_kernel(recv, mu, high, low, local, sums, work, extra):
    lane16 = lax.broadcasted_iota(jnp.int32, (KS, 128), 1)
    lane8 = lax.broadcasted_iota(jnp.int32, (8, 128), 1)
    for t in range(4):
        for group in range(4):
            pieces = [recv[4 * group + c, t * KS : (t + 1) * KS, :] for c in range(4)]
            for i, piece in enumerate(exchange(pieces, 32, lane16)):
                x = 4 * t + i
                work[x * KS : (x + 1) * KS, group * 128 : (group + 1) * 128] = piece
    extras = [recv[c, 4 * KS :, :] for c in range(SPAN)]
    for kt in range(2):
        for group in range(4):
            total = None
            for c in range(4):
                piece = pltpu.roll(extras[4 * group + c], (32 * c - 64 * kt) % 128, 1) if (32 * c - 64 * kt) % 128 else extras[4 * group + c]
                total = piece if total is None else jnp.where(lane8 // 32 == c, piece, total)
            at = BX * KS + kt * 8
            work[at : at + 8, group * 128 : (group + 1) * 128] = total
    for x, piece in enumerate(exchange(extras, 1, lane8)):
        extra[x * KS : x * KS + 8, :] = piece
        extra[x * KS + 8 : (x + 1) * KS, :] = pltpu.roll(piece, 64, 1)
    extra[BX * KS :, :] = jnp.zeros((KS, 128), f32)
    lower, upper = work[:, :HALF], work[:, HALF:]
    beyond = split(extra[...])
    for part in range(2):
        columns = slice(part * HALF, (part + 1) * HALF)
        folded = split(lower - upper if part else lower + upper)
        main = dot3(folded, (high[:HALF, columns], low[:HALF, columns]), NN)
        rest = dot3(beyond, (high[HALF:, columns], low[HALF:, columns]), NN)
        work[:, columns] = main + rest
    _, ratio = decay(mu[...])
    state = None
    for x in range(XR):
        value = work[x * KS : (x + 1) * KS, :]
        if state is not None:
            local[x * KS : (x + 1) * KS, :] = ratio * state
            state = value + ratio * state
        else:
            local[:KS, :] = jnp.zeros((KS, NY), f32)
            state = value
    ahead = None
    for x in range(XR - 1, -1, -1):
        value = work[x * KS : (x + 1) * KS, :]
        ahead = value if ahead is None else value + ratio * ahead
        local[x * KS : (x + 1) * KS, :] += ahead
    for kind, value in enumerate((state, ahead)):
        for kt in range(4):
            for mt in range(4):
                sums[kind * 16 + kt * 4 + mt] = value[4 * kt : 4 * kt + 4, 128 * mt : 128 * (mt + 1)]


def transform(recv, mu, high, low):
    vmem = pl.BlockSpec(memory_space=pltpu.VMEM)
    return pl.pallas_call(
        transform_kernel,
        in_specs=[vmem] * 4,
        out_specs=[vmem] * 2,
        out_shape=[
            jax.ShapeDtypeStruct((XR * KS, NY), f32),
            jax.ShapeDtypeStruct((AISLE, 4, 128), f32),
        ],
        scratch_shapes=[pltpu.VMEM((XR * KS, NY), f32), pltpu.VMEM((XR * KS, 128), f32)],
        name="transform",
    )(recv, mu, high, low)


def carry_kernel(kind, sums, mu, carries):
    backwards = kind[0]
    _, ratio = decay(mu[...])
    step = ratio
    for _ in range(4):
        step = step * step
    around = step
    for _ in range(5):
        around = around * around

    def place(i):
        return i + backwards * (AISLE - 1 - 2 * i)

    def gather(i, state):
        return sums[place(i)] + step * state

    state = lax.fori_loop(0, AISLE, gather, jnp.zeros_like(step), unroll=8) / (1.0 - around)

    def spread(i, state):
        at = place(i)
        carries[at] = state
        return sums[at] + step * state

    lax.fori_loop(0, AISLE, spread, state, unroll=8)


def carry(kind, sums, mu):
    vmem = pl.BlockSpec(memory_space=pltpu.VMEM)
    return pl.pallas_call(
        carry_kernel,
        in_specs=[pl.BlockSpec(memory_space=pltpu.SMEM), vmem, vmem],
        out_specs=vmem,
        out_shape=jax.ShapeDtypeStruct((AISLE, 4, 128), f32),
        name="carry",
    )(kind, sums, mu)


def inverse_kernel(local, carries, mu, weight, high, low, chunk, ends, work_high, work_low, work, extra):
    lane16 = lax.broadcasted_iota(jnp.int32, (KS, 128), 1)
    lane8 = lax.broadcasted_iota(jnp.int32, (8, 128), 1)
    for kind in range(2):
        for kt in range(4):
            for mt in range(4):
                ends[kind, 4 * kt : 4 * kt + 4, 128 * mt : 128 * (mt + 1)] = carries[kind * 16 + kt * 4 + mt]
    root, ratio = decay(mu[...])
    scale = -0.5 * weight[...] / root
    powers = [jnp.ones_like(ratio)]
    behind, ahead = ends[0], ends[1]
    backs = [ahead]
    for x in range(BX):
        backs.append(ratio * backs[-1])
    for x in range(XR):
        rows = slice(x * KS, (x + 1) * KS)
        value = split(scale * (local[rows, :] + behind + backs[BX - x]))
        work_high[rows, :] = value[0]
        work_low[rows, :] = value[1]
        behind = ratio * behind
    parts = []
    for part in range(2):
        columns = slice(part * HALF, (part + 1) * HALF)
        value = (work_high[:, columns], work_low[:, columns])
        parts.append(
            (
                dot3(value, (high[:HALF, columns], low[:HALF, columns]), NT),
                dot3(value, (high[HALF:, columns], low[HALF:, columns]), NT),
            )
        )
    work[:, :HALF] = parts[0][0] + parts[1][0]
    work[:, HALF:] = parts[0][0] - parts[1][0]
    extra[...] = parts[0][1] + parts[1][1]
    for t in range(4):
        for group in range(4):
            pieces = [work[x * KS : (x + 1) * KS, group * 128 : (group + 1) * 128] for x in range(4 * t, 4 * t + 4)]
            for i, piece in enumerate(exchange(pieces, 32, lane16)):
                chunk[4 * group + i, t * KS : (t + 1) * KS, :] = piece
    edges = []
    for x in range(BX):
        edges.append(
            jnp.where(lane8 < 64, extra[x * KS : x * KS + 8, :], pltpu.roll(extra[x * KS + 8 : (x + 1) * KS, :], 64, 1))
        )
    for c, piece in enumerate(exchange(edges, 1, lane8)):
        group, i = divmod(c, 4)
        for kt in range(2):
            at = BX * KS + kt * 8
            last = work[at : at + 8, group * 128 : (group + 1) * 128]
            turn = (64 * kt - 32 * i) % 128
            last = pltpu.roll(last, turn, 1) if turn else last
            piece = jnp.where(lane8 // 32 == 2 * kt, last, piece)
        chunk[c, 4 * KS :, :] = piece


def inverse(local, carries, mu, weight, high, low):
    vmem = pl.BlockSpec(memory_space=pltpu.VMEM)
    return pl.pallas_call(
        inverse_kernel,
        in_specs=[vmem] * 6,
        out_specs=vmem,
        out_shape=jax.ShapeDtypeStruct((SPAN, ROWS, 128), f32),
        scratch_shapes=[
            pltpu.VMEM((2, KS, NY), f32),
            pltpu.VMEM((XR * KS, NY), bf16),
            pltpu.VMEM((XR * KS, NY), bf16),
            pltpu.VMEM((XR * KS, NY), f32),
            pltpu.VMEM((XR * KS, 128), f32),
        ],
        name="inverse",
    )(local, carries, mu, weight, high, low)


def correct_kernel(recv, basis, es, ns, us, east, north, upward, press):
    back = split(basis[...])
    for t in range(4):
        modes = split(recv[:, t * KS : (t + 1) * KS, :].reshape(NZ, 128))
        press[t * 128 : (t + 1) * 128, :] = dot3(back, modes, NN).T
    extras = []
    for s in range(SPAN):
        piece = recv[s, 4 * KS :, :]
        extras.append(piece)
        extras.append(pltpu.roll(piece, 64, 1))
    modes = split(jnp.concatenate(extras, axis=0))
    press[512:640, :] = dot3(back, modes, NN).T
    row = lax.broadcasted_iota(jnp.int32, (BY, NZ), 0)
    lane = lax.broadcasted_iota(jnp.int32, (BY, NZ), 1)

    def plane(x, here):
        beyond = press[pl.ds(pl.multiple_of((x + 1) * BY, BY), BY), :]
        edge = press[pl.ds(BX * BY + BY + x, 1), :]
        beside = jnp.where(row == BY - 1, edge, pltpu.roll(here, BY - 1, 0))
        above = jnp.where(lane == NZ - 1, 0.0, pltpu.roll(here, NZ - 1, 1))
        east[x] = es[x] - (beyond - here)
        north[x] = ns[x] - (beside - here)
        upward[x] = us[x] - (above - here)
        return beyond

    lax.fori_loop(0, BX, plane, press[:BY, :])


def correct(recv, basis, es, ns, us):
    vmem = pl.BlockSpec(memory_space=pltpu.VMEM)
    block = jax.ShapeDtypeStruct((BX, BY, NZ), f32)
    return pl.pallas_call(
        correct_kernel,
        in_specs=[vmem] * 5,
        out_specs=[vmem] * 3,
        out_shape=[block] * 3,
        scratch_shapes=[pltpu.VMEM((BX * BY + 128, NZ), f32)],
        name="correct",
    )(recv, basis, es, ns, us)


def ring(axis, count, step, value):
    return lax.ppermute(value, axis, [(i, (i + step) % count) for i in range(count)])


def per_device(
    downflow_motion,
    crossflow_motion,
    upright_motion,
    thermal_anomaly,
    height_to_eigenbasis,
    eigenbasis_to_height,
    negated_height_spectrum,
):
    fields = (downflow_motion, crossflow_motion, upright_motion, thermal_anomaly)
    x_first, x_last, y_first, y_last = pack(fields)
    xlo = ring("aisle", AISLE, 1, x_last)
    xhi = ring("aisle", AISLE, -1, x_first)
    ylo = ring("span", SPAN, 1, y_last)
    yhi = ring("span", SPAN, -1, y_first)
    share = lax.dynamic_slice(negated_height_spectrum, (lax.axis_index("span") * KS,), (KS,))
    mu = share[:, None] + jnp.asarray(EIGEN)[None, :]
    turn = lax.axis_index("aisle")
    mu_lines = lax.dynamic_slice(mu, ((turn // 4) % 4 * 4, turn % 4 * 128), (4, 128))
    kind = (turn // 16).astype(jnp.int32).reshape(1)
    high, low = jnp.asarray(TABLE_HIGH), jnp.asarray(TABLE_LOW)
    weight = jnp.asarray(WEIGHT).reshape(1, NY)
    swap = functools.partial(lax.all_to_all, split_axis=0, concat_axis=0, tiled=True)
    es, ns, us, heat, chunk = predict(fields, xlo, xhi, ylo, yhi, height_to_eigenbasis)
    local, sums = transform(swap(chunk, "span"), mu, high, low)
    carries = carry(kind, swap(sums, "aisle"), mu_lines)
    chunk = inverse(local, swap(carries, "aisle"), mu, weight, high, low)
    east, north, upward = correct(swap(chunk, "span"), eigenbasis_to_height, es, ns, us)
    return (east, north, upward, heat)


def solution(mesh):
    block = P("aisle", "span", None)
    return jax.shard_map(
        per_device,
        mesh=mesh,
        in_specs=(block,) * 4 + (P(), P(), P()),
        out_specs=(block,) * 4,
        check_vma=False,
    )
```

```python
import functools
import math

import jax
import jax.numpy as jnp
import ml_dtypes
import numpy as np
from jax import lax
from jax.experimental import pallas as pl
from jax.experimental.pallas import tpu as pltpu
from jax.sharding import PartitionSpec as P

f32 = jnp.float32
bf16 = jnp.bfloat16
step_gain = 0.1 * 8.0 / 15.0
viscosity = 0.01
smagorinsky = 0.05
prandtl = 0.7
buoyancy = 1.0
strain_floor = 0.25

AISLE = 32
SPAN = 16
BX = 16
BY = 32
NZ = 256
NY = SPAN * BY
KS = NZ // SPAN
HALF = NY // 2
XR = BX + 1
ROWS = 72


def y_tables():
    cells = np.arange(HALF)
    even = [(m, 0) for m in range(0, HALF + 1, 2)] + [(m, 1) for m in range(2, HALF, 2)]
    odd = [(m, 0) for m in range(1, HALF, 2)] + [(m, 1) for m in range(1, HALF, 2)]
    modes = even + odd
    edges = (BY * (np.arange(SPAN) + 1)) % NY

    def rows(at):
        wave = np.array([m for m, _ in modes])
        odd_part = np.array([s for _, s in modes])
        angle = 2.0 * np.pi / NY * ((at[:, None] * wave[None, :]) % NY)
        return np.where(odd_part[None, :] == 1, np.sin(angle), np.cos(angle))

    main = rows(cells)
    extra = np.zeros((128, NY))
    extra[32 : 32 + SPAN] = rows(edges)
    table = np.concatenate([main, extra], axis=0).astype(np.float32)
    high = table.astype(ml_dtypes.bfloat16)
    low = (table - high.astype(np.float32)).astype(ml_dtypes.bfloat16)
    wave = np.array([m for m, _ in modes])
    eigen = (4.0 * np.sin(np.pi * wave / NY) ** 2).astype(np.float32)
    weight = np.where((wave == 0) | (wave == HALF), 1.0 / NY, 2.0 / NY).astype(np.float32)
    return high, low, eigen, weight


TABLE_HIGH, TABLE_LOW, EIGEN, WEIGHT = y_tables()


def split(value):
    high = value.astype(bf16)
    low = (value - high.astype(f32)).astype(bf16)
    return high, low


def dot3(a, b, dims):
    def one(p, q):
        return lax.dot_general(p, q, (dims, ((), ())), preferred_element_type=f32)

    return one(a[0], b[0]) + (one(a[0], b[1]) + one(a[1], b[0]))


NN = ((1,), (0,))
NT = ((1,), (1,))


def exchange(vectors, unit, lane):
    vectors = list(vectors)
    distance = len(vectors) // 2
    while distance:
        upper = (lane // (unit * distance)) % 2 == 1
        for i in range(len(vectors)):
            if i & distance:
                continue
            a, b = vectors[i], vectors[i + distance]
            vectors[i] = jnp.where(upper, pltpu.roll(b, unit * distance, 1), a)
            vectors[i + distance] = jnp.where(upper, b, pltpu.roll(a, 128 - unit * distance, 1))
        distance //= 2
    return vectors


def near(value):
    return pltpu.with_memory_space_constraint(value, pltpu.VMEM)


def pack_kernel(*refs):
    x_first, x_last, y_first, y_last = refs[16:]
    for f in range(4):
        x_first[f] = refs[f][0]
        x_last[f] = refs[4 + f][0]
        y_first[f] = refs[8 + f][:, 0, :]
        y_last[f] = refs[12 + f][:, 7, :]


def pack(fields):
    plane = lambda at: pl.BlockSpec((1, BY, NZ), lambda i: (at, 0, 0))
    rows = lambda at: pl.BlockSpec((BX, 8, NZ), lambda i: (0, at, 0))
    whole = lambda shape: pl.BlockSpec(shape, lambda i: (0, 0, 0))
    xs, ys = (4, BY, NZ), (4, BX, NZ)
    return pl.pallas_call(
        pack_kernel,
        grid=(1,),
        in_specs=[plane(0)] * 4 + [plane(BX - 1)] * 4 + [rows(0)] * 4 + [rows(BY // 8 - 1)] * 4,
        out_specs=[whole(xs), whole(xs), whole(ys), whole(ys)],
        out_shape=[jax.ShapeDtypeStruct(s, f32) for s in (xs, xs, ys, ys)],
        name="pack",
    )(*fields, *fields, *fields, *fields)


def predict_kernel(
    fd, fc, fu, ft, xlo, xhi, ylo, yhi, basis, es, ns, us, ts, chunk, buf, src, out, sems, done
):
    loads = []
    for t in range(4):
        first, last = (4 * t + 1 if t else 0), min(4 * t + 5, BX)
        loads.append(
            [
                pltpu.make_async_copy(
                    f.at[pl.ds(first, last - first)], buf.at[i, pl.ds(first + 1, last - first)], sems.at[t, i]
                )
                for i, f in enumerate((fd, fc, fu, ft))
            ]
        )
        for copy in loads[t]:
            copy.start()
    buf[:, 0] = xlo[...]
    buf[:, BX + 1] = xhi[...]
    row = lax.broadcasted_iota(jnp.int32, (BY, NZ), 0)
    lane = lax.broadcasted_iota(jnp.int32, (BY, NZ), 1)
    base = BX * BY
    src[base + BY :, :] = jnp.zeros((128 - BY, NZ), f32)
    zero = jnp.zeros((BY, NZ), f32)

    def south_of(value, edge):
        return jnp.where(row == 0, edge, pltpu.roll(value, 1, 0))

    def lower_of(value):
        return jnp.where(lane == 0, 0.0, pltpu.roll(value, 1, 1))

    def plane(x, east_prev):
        centre, steps, laplace = [], [], []
        for f in range(4):
            c = buf[f, x + 1]
            w, e = buf[f, x], buf[f, x + 2]
            s = south_of(c, ylo[f, pl.ds(x, 1), :])
            n = jnp.where(row == BY - 1, yhi[f, pl.ds(x, 1), :], pltpu.roll(c, BY - 1, 0))
            l = lower_of(c)
            u = jnp.where(lane == NZ - 1, 0.0, pltpu.roll(c, NZ - 1, 1))
            centre.append(c)
            steps.append((e - w, n - s, u - l))
            laplace.append((e + w) + (n + s) + (u + l) - 6.0 * c)
        strain = sum(d * d for f in range(3) for d in steps[f])
        turbulent = viscosity + smagorinsky * jnp.sqrt(0.25 * strain + strain_floor)
        stars = []
        for f in range(4):
            k = turbulent if f < 3 else turbulent * (1.0 / prandtl)
            dx, dy, dz = steps[f]
            transport = 0.5 * (centre[0] * dx + centre[1] * dy + centre[2] * dz)
            tendency = k * laplace[f] - transport
            if f == 2:
                tendency = tendency + buoyancy * centre[3]
            stars.append(centre[f] + step_gain * tendency)
        east, north, upward, heat = stars
        for f in range(4):
            out[f, x] = stars[f]
        flux = (east - east_prev) + (north - south_of(north, zero)) + (upward - lower_of(upward))
        src[pl.ds(pl.multiple_of(x * BY, BY), BY), :] = flux
        src[pl.ds(base + BY + x, 1), :] = -north[BY - 1 :, :]
        return east

    last = zero
    stores = []
    for t in range(4):
        for copy in loads[t]:
            copy.wait()
        last = lax.fori_loop(4 * t, 4 * t + 4, plane, last)
        for f, ref in enumerate((es, ns, us, ts)):
            copy = pltpu.make_async_copy(out.at[f, pl.ds(4 * t, 4)], ref.at[pl.ds(4 * t, 4)], done.at[t, f])
            copy.start()
            stores.append(copy)
    src[base : base + BY, :] = -last
    forward = split(basis[...])
    for t in range(5):
        modes = dot3(forward, split(src[t * 128 : (t + 1) * 128, :]), NT)
        if t < 4:
            chunk[:, t * KS : (t + 1) * KS, :] = modes.reshape(SPAN, KS, 128)
        else:
            modes = modes.reshape(SPAN, 2, 8, 128)
            lanes = lax.broadcasted_iota(jnp.int32, (8, 128), 1)
            for s in range(SPAN):
                chunk[s, 4 * KS :, :] = jnp.where(lanes < 64, modes[s, 0], pltpu.roll(modes[s, 1], 64, 1))
    for copy in stores:
        copy.wait()


def predict(fields, xlo, xhi, ylo, yhi, basis):
    any_spec = pl.BlockSpec(memory_space=pl.ANY)
    vmem = pl.BlockSpec(memory_space=pltpu.VMEM)
    block = jax.ShapeDtypeStruct((BX, BY, NZ), f32)
    return pl.pallas_call(
        predict_kernel,
        in_specs=[any_spec] * 4 + [vmem] * 5,
        out_specs=[any_spec] * 4 + [vmem],
        out_shape=[block] * 4 + [jax.ShapeDtypeStruct((SPAN, ROWS, 128), f32)],
        scratch_shapes=[
            pltpu.VMEM((4, BX + 2, BY, NZ), f32),
            pltpu.VMEM((BX * BY + 128, NZ), f32),
            pltpu.VMEM((4, BX, BY, NZ), f32),
            pltpu.SemaphoreType.DMA((4, 4)),
            pltpu.SemaphoreType.DMA((4, 4)),
        ],
        name="predict",
    )(*fields, near(xlo), near(xhi), near(ylo), near(yhi), basis)


def decay(mu):
    root = jnp.sqrt(mu + 0.25 * mu * mu)
    return root, 1.0 / (1.0 + 0.5 * mu + root)


def transform_kernel(recv, mu, high, low, local, sums, work, extra):
    lane16 = lax.broadcasted_iota(jnp.int32, (KS, 128), 1)
    lane8 = lax.broadcasted_iota(jnp.int32, (8, 128), 1)
    for t in range(4):
        for group in range(4):
            pieces = [recv[4 * group + c, t * KS : (t + 1) * KS, :] for c in range(4)]
            for i, piece in enumerate(exchange(pieces, 32, lane16)):
                x = 4 * t + i
                work[x * KS : (x + 1) * KS, group * 128 : (group + 1) * 128] = piece
    extras = [recv[c, 4 * KS :, :] for c in range(SPAN)]
    for kt in range(2):
        for group in range(4):
            total = None
            for c in range(4):
                piece = pltpu.roll(extras[4 * group + c], (32 * c - 64 * kt) % 128, 1) if (32 * c - 64 * kt) % 128 else extras[4 * group + c]
                total = piece if total is None else jnp.where(lane8 // 32 == c, piece, total)
            at = BX * KS + kt * 8
            work[at : at + 8, group * 128 : (group + 1) * 128] = total
    for x, piece in enumerate(exchange(extras, 1, lane8)):
        extra[x * KS : x * KS + 8, :] = piece
        extra[x * KS + 8 : (x + 1) * KS, :] = pltpu.roll(piece, 64, 1)
    extra[BX * KS :, :] = jnp.zeros((KS, 128), f32)
    lower, upper = work[:, :HALF], work[:, HALF:]
    beyond = split(extra[...])
    for part in range(2):
        columns = slice(part * HALF, (part + 1) * HALF)
        folded = split(lower - upper if part else lower + upper)
        main = dot3(folded, (high[:HALF, columns], low[:HALF, columns]), NN)
        rest = dot3(beyond, (high[HALF:, columns], low[HALF:, columns]), NN)
        work[:, columns] = main + rest
    _, ratio = decay(mu[...])
    state = None
    for x in range(XR):
        value = work[x * KS : (x + 1) * KS, :]
        if state is not None:
            local[x * KS : (x + 1) * KS, :] = ratio * state
            state = value + ratio * state
        else:
            local[:KS, :] = jnp.zeros((KS, NY), f32)
            state = value
    ahead = None
    for x in range(XR - 1, -1, -1):
        value = work[x * KS : (x + 1) * KS, :]
        ahead = value if ahead is None else value + ratio * ahead
        local[x * KS : (x + 1) * KS, :] += ahead
    for kind, value in enumerate((state, ahead)):
        for kt in range(4):
            for mt in range(4):
                sums[kind * 16 + kt * 4 + mt] = value[4 * kt : 4 * kt + 4, 128 * mt : 128 * (mt + 1)]


def transform(recv, mu, high, low):
    vmem = pl.BlockSpec(memory_space=pltpu.VMEM)
    return pl.pallas_call(
        transform_kernel,
        in_specs=[vmem] * 4,
        out_specs=[vmem] * 2,
        out_shape=[
            jax.ShapeDtypeStruct((XR * KS, NY), f32),
            jax.ShapeDtypeStruct((AISLE, 4, 128), f32),
        ],
        scratch_shapes=[pltpu.VMEM((XR * KS, NY), f32), pltpu.VMEM((XR * KS, 128), f32)],
        name="transform",
    )(near(recv), mu, high, low)


def carry_kernel(kind, sums, mu, carries):
    backwards = kind[0]
    _, ratio = decay(mu[...])
    step = ratio
    for _ in range(4):
        step = step * step
    around = step
    for _ in range(5):
        around = around * around

    def place(i):
        return i + backwards * (AISLE - 1 - 2 * i)

    def gather(i, state):
        return sums[place(i)] + step * state

    state = lax.fori_loop(0, AISLE, gather, jnp.zeros_like(step), unroll=8) / (1.0 - around)

    def spread(i, state):
        at = place(i)
        carries[at] = state
        return sums[at] + step * state

    lax.fori_loop(0, AISLE, spread, state, unroll=8)


def carry(kind, sums, mu):
    vmem = pl.BlockSpec(memory_space=pltpu.VMEM)
    return pl.pallas_call(
        carry_kernel,
        in_specs=[pl.BlockSpec(memory_space=pltpu.SMEM), vmem, vmem],
        out_specs=vmem,
        out_shape=jax.ShapeDtypeStruct((AISLE, 4, 128), f32),
        name="carry",
    )(kind, near(sums), mu)


def inverse_kernel(local, carries, mu, weight, high, low, chunk, ends, work_high, work_low, work, extra):
    lane16 = lax.broadcasted_iota(jnp.int32, (KS, 128), 1)
    lane8 = lax.broadcasted_iota(jnp.int32, (8, 128), 1)
    for kind in range(2):
        for kt in range(4):
            for mt in range(4):
                ends[kind, 4 * kt : 4 * kt + 4, 128 * mt : 128 * (mt + 1)] = carries[kind * 16 + kt * 4 + mt]
    root, ratio = decay(mu[...])
    scale = -0.5 * weight[...] / root
    powers = [jnp.ones_like(ratio)]
    behind, ahead = ends[0], ends[1]
    backs = [ahead]
    for x in range(BX):
        backs.append(ratio * backs[-1])
    for x in range(XR):
        rows = slice(x * KS, (x + 1) * KS)
        value = split(scale * (local[rows, :] + behind + backs[BX - x]))
        work_high[rows, :] = value[0]
        work_low[rows, :] = value[1]
        behind = ratio * behind
    parts = []
    for part in range(2):
        columns = slice(part * HALF, (part + 1) * HALF)
        value = (work_high[:, columns], work_low[:, columns])
        parts.append(
            (
                dot3(value, (high[:HALF, columns], low[:HALF, columns]), NT),
                dot3(value, (high[HALF:, columns], low[HALF:, columns]), NT),
            )
        )
    work[:, :HALF] = parts[0][0] + parts[1][0]
    work[:, HALF:] = parts[0][0] - parts[1][0]
    extra[...] = parts[0][1] + parts[1][1]
    for t in range(4):
        for group in range(4):
            pieces = [work[x * KS : (x + 1) * KS, group * 128 : (group + 1) * 128] for x in range(4 * t, 4 * t + 4)]
            for i, piece in enumerate(exchange(pieces, 32, lane16)):
                chunk[4 * group + i, t * KS : (t + 1) * KS, :] = piece
    edges = []
    for x in range(BX):
        edges.append(
            jnp.where(lane8 < 64, extra[x * KS : x * KS + 8, :], pltpu.roll(extra[x * KS + 8 : (x + 1) * KS, :], 64, 1))
        )
    for c, piece in enumerate(exchange(edges, 1, lane8)):
        group, i = divmod(c, 4)
        for kt in range(2):
            at = BX * KS + kt * 8
            last = work[at : at + 8, group * 128 : (group + 1) * 128]
            turn = (64 * kt - 32 * i) % 128
            last = pltpu.roll(last, turn, 1) if turn else last
            piece = jnp.where(lane8 // 32 == 2 * kt, last, piece)
        chunk[c, 4 * KS :, :] = piece


def inverse(local, carries, mu, weight, high, low):
    vmem = pl.BlockSpec(memory_space=pltpu.VMEM)
    return pl.pallas_call(
        inverse_kernel,
        in_specs=[vmem] * 6,
        out_specs=vmem,
        out_shape=jax.ShapeDtypeStruct((SPAN, ROWS, 128), f32),
        scratch_shapes=[
            pltpu.VMEM((2, KS, NY), f32),
            pltpu.VMEM((XR * KS, NY), bf16),
            pltpu.VMEM((XR * KS, NY), bf16),
            pltpu.VMEM((XR * KS, NY), f32),
            pltpu.VMEM((XR * KS, 128), f32),
        ],
        name="inverse",
    )(local, near(carries), mu, weight, high, low)


def correct_kernel(recv, basis, es, ns, us, east, north, upward, press, buf, sems, done):
    loads = [pltpu.make_async_copy(ref, buf.at[f], sems.at[f]) for f, ref in enumerate((es, ns, us))]
    for copy in loads:
        copy.start()
    back = split(basis[...])
    for t in range(4):
        modes = split(recv[:, t * KS : (t + 1) * KS, :].reshape(NZ, 128))
        press[t * 128 : (t + 1) * 128, :] = dot3(back, modes, NN).T
    extras = []
    for s in range(SPAN):
        piece = recv[s, 4 * KS :, :]
        extras.append(piece)
        extras.append(pltpu.roll(piece, 64, 1))
    modes = split(jnp.concatenate(extras, axis=0))
    press[512:640, :] = dot3(back, modes, NN).T
    row = lax.broadcasted_iota(jnp.int32, (BY, NZ), 0)
    lane = lax.broadcasted_iota(jnp.int32, (BY, NZ), 1)

    def plane(x, here):
        beyond = press[pl.ds(pl.multiple_of((x + 1) * BY, BY), BY), :]
        edge = press[pl.ds(BX * BY + BY + x, 1), :]
        beside = jnp.where(row == BY - 1, edge, pltpu.roll(here, BY - 1, 0))
        above = jnp.where(lane == NZ - 1, 0.0, pltpu.roll(here, NZ - 1, 1))
        for f, value in enumerate((beyond, beside, above)):
            buf[f, x] = buf[f, x] - (value - here)
        return beyond

    for copy in loads:
        copy.wait()
    here = press[:BY, :]
    stores = []
    for t in range(4):
        here = lax.fori_loop(4 * t, 4 * t + 4, plane, here)
        for f, ref in enumerate((east, north, upward)):
            copy = pltpu.make_async_copy(buf.at[f, pl.ds(4 * t, 4)], ref.at[pl.ds(4 * t, 4)], done.at[t, f])
            copy.start()
            stores.append(copy)
    for copy in stores:
        copy.wait()


def correct(recv, basis, es, ns, us):
    any_spec = pl.BlockSpec(memory_space=pl.ANY)
    vmem = pl.BlockSpec(memory_space=pltpu.VMEM)
    block = jax.ShapeDtypeStruct((BX, BY, NZ), f32)
    return pl.pallas_call(
        correct_kernel,
        in_specs=[vmem] * 2 + [any_spec] * 3,
        out_specs=[any_spec] * 3,
        out_shape=[block] * 3,
        scratch_shapes=[
            pltpu.VMEM((BX * BY + 128, NZ), f32),
            pltpu.VMEM((3, BX, BY, NZ), f32),
            pltpu.SemaphoreType.DMA((3,)),
            pltpu.SemaphoreType.DMA((4, 3)),
        ],
        name="correct",
    )(near(recv), basis, es, ns, us)


def ring(axis, count, step, value):
    return lax.ppermute(value, axis, [(i, (i + step) % count) for i in range(count)])


def per_device(
    downflow_motion,
    crossflow_motion,
    upright_motion,
    thermal_anomaly,
    height_to_eigenbasis,
    eigenbasis_to_height,
    negated_height_spectrum,
):
    fields = (downflow_motion, crossflow_motion, upright_motion, thermal_anomaly)
    x_first, x_last, y_first, y_last = pack(fields)
    xlo = ring("aisle", AISLE, 1, x_last)
    xhi = ring("aisle", AISLE, -1, x_first)
    ylo = ring("span", SPAN, 1, y_last)
    yhi = ring("span", SPAN, -1, y_first)
    share = lax.dynamic_slice(negated_height_spectrum, (lax.axis_index("span") * KS,), (KS,))
    mu = share[:, None] + jnp.asarray(EIGEN)[None, :]
    turn = lax.axis_index("aisle")
    mu_lines = lax.dynamic_slice(mu, ((turn // 4) % 4 * 4, turn % 4 * 128), (4, 128))
    kind = (turn // 16).astype(jnp.int32).reshape(1)
    high, low = jnp.asarray(TABLE_HIGH), jnp.asarray(TABLE_LOW)
    weight = jnp.asarray(WEIGHT).reshape(1, NY)
    swap = functools.partial(lax.all_to_all, split_axis=0, concat_axis=0, tiled=True)
    es, ns, us, heat, chunk = predict(fields, xlo, xhi, ylo, yhi, height_to_eigenbasis)
    local, sums = transform(swap(chunk, "span"), mu, high, low)
    carries = carry(kind, swap(sums, "aisle"), mu_lines)
    chunk = inverse(local, swap(carries, "aisle"), mu, weight, high, low)
    east, north, upward = correct(swap(chunk, "span"), eigenbasis_to_height, es, ns, us)
    return (east, north, upward, heat)


def solution(mesh):
    block = P("aisle", "span", None)
    return jax.shard_map(
        per_device,
        mesh=mesh,
        in_specs=(block,) * 4 + (P(), P(), P()),
        out_specs=(block,) * 4,
        check_vma=False,
    )
```

```python
import functools
import math

import jax
import jax.numpy as jnp
import ml_dtypes
import numpy as np
from jax import lax
from jax.experimental import pallas as pl
from jax.experimental.pallas import tpu as pltpu
from jax.sharding import PartitionSpec as P

f32 = jnp.float32
bf16 = jnp.bfloat16
step_gain = 0.1 * 8.0 / 15.0
viscosity = 0.01
smagorinsky = 0.05
prandtl = 0.7
buoyancy = 1.0
strain_floor = 0.25

AISLE = 32
SPAN = 16
BX = 16
BY = 32
NZ = 256
NY = SPAN * BY
KS = NZ // SPAN
HALF = NY // 2
XR = BX + 1
ROWS = 72


def y_tables():
    cells = np.arange(HALF)
    even = [(m, 0) for m in range(0, HALF + 1, 2)] + [(m, 1) for m in range(2, HALF, 2)]
    odd = [(m, 0) for m in range(1, HALF, 2)] + [(m, 1) for m in range(1, HALF, 2)]
    modes = even + odd
    edges = (BY * (np.arange(SPAN) + 1)) % NY

    def rows(at):
        wave = np.array([m for m, _ in modes])
        odd_part = np.array([s for _, s in modes])
        angle = 2.0 * np.pi / NY * ((at[:, None] * wave[None, :]) % NY)
        return np.where(odd_part[None, :] == 1, np.sin(angle), np.cos(angle))

    main = rows(cells)
    extra = np.zeros((128, NY))
    extra[32 : 32 + SPAN] = rows(edges)
    table = np.concatenate([main, extra], axis=0).astype(np.float32)
    high = table.astype(ml_dtypes.bfloat16)
    low = (table - high.astype(np.float32)).astype(ml_dtypes.bfloat16)
    wave = np.array([m for m, _ in modes])
    eigen = (4.0 * np.sin(np.pi * wave / NY) ** 2).astype(np.float32)
    weight = np.where((wave == 0) | (wave == HALF), 1.0 / NY, 2.0 / NY).astype(np.float32)
    return high, low, eigen, weight


TABLE_HIGH, TABLE_LOW, EIGEN, WEIGHT = y_tables()


def split(value):
    high = value.astype(bf16)
    low = (value - high.astype(f32)).astype(bf16)
    return high, low


def dot3(a, b, dims):
    def one(p, q):
        return lax.dot_general(p, q, (dims, ((), ())), preferred_element_type=f32)

    return one(a[0], b[0]) + (one(a[0], b[1]) + one(a[1], b[0]))


NN = ((1,), (0,))
NT = ((1,), (1,))


def exchange(vectors, unit, lane):
    vectors = list(vectors)
    distance = len(vectors) // 2
    while distance:
        upper = (lane // (unit * distance)) % 2 == 1
        for i in range(len(vectors)):
            if i & distance:
                continue
            a, b = vectors[i], vectors[i + distance]
            vectors[i] = jnp.where(upper, pltpu.roll(b, unit * distance, 1), a)
            vectors[i + distance] = jnp.where(upper, b, pltpu.roll(a, 128 - unit * distance, 1))
        distance //= 2
    return vectors


def near(value):
    return pltpu.with_memory_space_constraint(value, pltpu.VMEM)


def pack_kernel(*refs):
    x_first, x_last, y_first, y_last = refs[16:]
    for f in range(4):
        x_first[f] = refs[f][0]
        x_last[f] = refs[4 + f][0]
        y_first[f] = refs[8 + f][:, 0, :]
        y_last[f] = refs[12 + f][:, 7, :]


def pack(fields):
    plane = lambda at: pl.BlockSpec((1, BY, NZ), lambda i: (at, 0, 0))
    rows = lambda at: pl.BlockSpec((BX, 8, NZ), lambda i: (0, at, 0))
    whole = lambda shape: pl.BlockSpec(shape, lambda i: (0, 0, 0))
    xs, ys = (4, BY, NZ), (4, BX, NZ)
    return pl.pallas_call(
        pack_kernel,
        grid=(1,),
        in_specs=[plane(0)] * 4 + [plane(BX - 1)] * 4 + [rows(0)] * 4 + [rows(BY // 8 - 1)] * 4,
        out_specs=[whole(xs), whole(xs), whole(ys), whole(ys)],
        out_shape=[jax.ShapeDtypeStruct(s, f32) for s in (xs, xs, ys, ys)],
        name="pack",
    )(*fields, *fields, *fields, *fields)


def predict_kernel(
    fd, fc, fu, ft, xlo, xhi, ylo, yhi, basis, es, ns, us, ts, chunk, buf, src, out, sems, done
):
    loads = []
    for t in range(4):
        first, last = (4 * t + 1 if t else 0), min(4 * t + 5, BX)
        loads.append(
            [
                pltpu.make_async_copy(
                    f.at[pl.ds(first, last - first)], buf.at[i, pl.ds(first + 1, last - first)], sems.at[t, i]
                )
                for i, f in enumerate((fd, fc, fu, ft))
            ]
        )
        for copy in loads[t]:
            copy.start()
    buf[:, 0] = xlo[...]
    buf[:, BX + 1] = xhi[...]
    row = lax.broadcasted_iota(jnp.int32, (BY, NZ), 0)
    lane = lax.broadcasted_iota(jnp.int32, (BY, NZ), 1)
    base = BX * BY
    src[base + BY :, :] = jnp.zeros((128 - BY, NZ), f32)
    zero = jnp.zeros((BY, NZ), f32)

    def south_of(value, edge):
        return jnp.where(row == 0, edge, pltpu.roll(value, 1, 0))

    def lower_of(value):
        return jnp.where(lane == 0, 0.0, pltpu.roll(value, 1, 1))

    def plane(x, east_prev):
        centre, steps, laplace = [], [], []
        for f in range(4):
            c = buf[f, x + 1]
            w, e = buf[f, x], buf[f, x + 2]
            s = south_of(c, ylo[f, pl.ds(x, 1), :])
            n = jnp.where(row == BY - 1, yhi[f, pl.ds(x, 1), :], pltpu.roll(c, BY - 1, 0))
            l = lower_of(c)
            u = jnp.where(lane == NZ - 1, 0.0, pltpu.roll(c, NZ - 1, 1))
            centre.append(c)
            steps.append((e - w, n - s, u - l))
            laplace.append((e + w) + (n + s) + (u + l) - 6.0 * c)
        strain = sum(d * d for f in range(3) for d in steps[f])
        turbulent = viscosity + smagorinsky * jnp.sqrt(0.25 * strain + strain_floor)
        stars = []
        for f in range(4):
            k = turbulent if f < 3 else turbulent * (1.0 / prandtl)
            dx, dy, dz = steps[f]
            transport = 0.5 * (centre[0] * dx + centre[1] * dy + centre[2] * dz)
            tendency = k * laplace[f] - transport
            if f == 2:
                tendency = tendency + buoyancy * centre[3]
            stars.append(centre[f] + step_gain * tendency)
        east, north, upward, heat = stars
        for f in range(4):
            out[f, x] = stars[f]
        flux = (east - east_prev) + (north - south_of(north, zero)) + (upward - lower_of(upward))
        src[pl.ds(pl.multiple_of(x * BY, BY), BY), :] = flux
        src[pl.ds(base + BY + x, 1), :] = -north[BY - 1 :, :]
        return east

    last = zero
    stores = []
    for t in range(4):
        for copy in loads[t]:
            copy.wait()
        last = lax.fori_loop(4 * t, 4 * t + 4, plane, last)
        for f, ref in enumerate((es, ns, us, ts)):
            copy = pltpu.make_async_copy(out.at[f, pl.ds(4 * t, 4)], ref.at[pl.ds(4 * t, 4)], done.at[t, f])
            copy.start()
            stores.append(copy)
    src[base : base + BY, :] = -last
    forward = split(basis[...])
    for t in range(5):
        modes = dot3(forward, split(src[t * 128 : (t + 1) * 128, :]), NT)
        if t < 4:
            chunk[:, t * KS : (t + 1) * KS, :] = modes.reshape(SPAN, KS, 128)
        else:
            modes = modes.reshape(SPAN, 2, 8, 128)
            lanes = lax.broadcasted_iota(jnp.int32, (8, 128), 1)
            for s in range(SPAN):
                chunk[s, 4 * KS :, :] = jnp.where(lanes < 64, modes[s, 0], pltpu.roll(modes[s, 1], 64, 1))
    for copy in stores:
        copy.wait()


def predict(fields, xlo, xhi, ylo, yhi, basis):
    any_spec = pl.BlockSpec(memory_space=pl.ANY)
    vmem = pl.BlockSpec(memory_space=pltpu.VMEM)
    block = jax.ShapeDtypeStruct((BX, BY, NZ), f32)
    return pl.pallas_call(
        predict_kernel,
        in_specs=[any_spec] * 4 + [vmem] * 5,
        out_specs=[any_spec] * 4 + [vmem],
        out_shape=[block] * 4 + [jax.ShapeDtypeStruct((SPAN, ROWS, 128), f32)],
        scratch_shapes=[
            pltpu.VMEM((4, BX + 2, BY, NZ), f32),
            pltpu.VMEM((BX * BY + 128, NZ), f32),
            pltpu.VMEM((4, BX, BY, NZ), f32),
            pltpu.SemaphoreType.DMA((4, 4)),
            pltpu.SemaphoreType.DMA((4, 4)),
        ],
        name="predict",
    )(*fields, near(xlo), near(xhi), near(ylo), near(yhi), near(basis))


def decay(mu):
    root = jnp.sqrt(mu + 0.25 * mu * mu)
    return root, 1.0 / (1.0 + 0.5 * mu + root)


def transform_kernel(recv, mu, high, low, local, sums, work, extra):
    lane16 = lax.broadcasted_iota(jnp.int32, (KS, 128), 1)
    lane8 = lax.broadcasted_iota(jnp.int32, (8, 128), 1)
    for t in range(4):
        for group in range(4):
            pieces = [recv[4 * group + c, t * KS : (t + 1) * KS, :] for c in range(4)]
            for i, piece in enumerate(exchange(pieces, 32, lane16)):
                x = 4 * t + i
                work[x * KS : (x + 1) * KS, group * 128 : (group + 1) * 128] = piece
    extras = [recv[c, 4 * KS :, :] for c in range(SPAN)]
    for kt in range(2):
        for group in range(4):
            total = None
            for c in range(4):
                piece = pltpu.roll(extras[4 * group + c], (32 * c - 64 * kt) % 128, 1) if (32 * c - 64 * kt) % 128 else extras[4 * group + c]
                total = piece if total is None else jnp.where(lane8 // 32 == c, piece, total)
            at = BX * KS + kt * 8
            work[at : at + 8, group * 128 : (group + 1) * 128] = total
    for x, piece in enumerate(exchange(extras, 1, lane8)):
        extra[x * KS : x * KS + 8, :] = piece
        extra[x * KS + 8 : (x + 1) * KS, :] = pltpu.roll(piece, 64, 1)
    extra[BX * KS :, :] = jnp.zeros((KS, 128), f32)
    lower, upper = work[:, :HALF], work[:, HALF:]
    beyond = split(extra[...])
    for part in range(2):
        columns = slice(part * HALF, (part + 1) * HALF)
        folded = split(lower - upper if part else lower + upper)
        main = dot3(folded, (high[:HALF, columns], low[:HALF, columns]), NN)
        rest = dot3(beyond, (high[HALF:, columns], low[HALF:, columns]), NN)
        work[:, columns] = main + rest
    _, ratio = decay(mu[...])
    state = None
    for x in range(XR):
        value = work[x * KS : (x + 1) * KS, :]
        if state is not None:
            local[x * KS : (x + 1) * KS, :] = ratio * state
            state = value + ratio * state
        else:
            local[:KS, :] = jnp.zeros((KS, NY), f32)
            state = value
    ahead = None
    for x in range(XR - 1, -1, -1):
        value = work[x * KS : (x + 1) * KS, :]
        ahead = value if ahead is None else value + ratio * ahead
        local[x * KS : (x + 1) * KS, :] += ahead
    for kind, value in enumerate((state, ahead)):
        for kt in range(4):
            for mt in range(4):
                sums[kind * 16 + kt * 4 + mt] = value[4 * kt : 4 * kt + 4, 128 * mt : 128 * (mt + 1)]


def transform(recv, mu, high, low):
    vmem = pl.BlockSpec(memory_space=pltpu.VMEM)
    return pl.pallas_call(
        transform_kernel,
        in_specs=[vmem] * 4,
        out_specs=[vmem] * 2,
        out_shape=[
            pltpu.VMEM((XR * KS, NY), f32),
            jax.ShapeDtypeStruct((AISLE, 4, 128), f32),
        ],
        scratch_shapes=[pltpu.VMEM((XR * KS, NY), f32), pltpu.VMEM((XR * KS, 128), f32)],
        name="transform",
    )(near(recv), near(mu), near(high), near(low))


def carry_kernel(kind, sums, mu, carries):
    backwards = kind[0]
    _, ratio = decay(mu[...])
    step = ratio
    for _ in range(4):
        step = step * step
    around = step
    for _ in range(5):
        around = around * around

    def place(i):
        return i + backwards * (AISLE - 1 - 2 * i)

    def gather(i, state):
        return sums[place(i)] + step * state

    state = lax.fori_loop(0, AISLE, gather, jnp.zeros_like(step), unroll=8) / (1.0 - around)

    def spread(i, state):
        at = place(i)
        carries[at] = state
        return sums[at] + step * state

    lax.fori_loop(0, AISLE, spread, state, unroll=8)


def carry(kind, sums, mu):
    vmem = pl.BlockSpec(memory_space=pltpu.VMEM)
    return pl.pallas_call(
        carry_kernel,
        in_specs=[pl.BlockSpec(memory_space=pltpu.SMEM), vmem, vmem],
        out_specs=vmem,
        out_shape=jax.ShapeDtypeStruct((AISLE, 4, 128), f32),
        name="carry",
    )(kind, near(sums), near(mu))


def inverse_kernel(local, carries, mu, weight, high, low, chunk, ends, work_high, work_low, work, extra):
    lane16 = lax.broadcasted_iota(jnp.int32, (KS, 128), 1)
    lane8 = lax.broadcasted_iota(jnp.int32, (8, 128), 1)
    for kind in range(2):
        for kt in range(4):
            for mt in range(4):
                ends[kind, 4 * kt : 4 * kt + 4, 128 * mt : 128 * (mt + 1)] = carries[kind * 16 + kt * 4 + mt]
    root, ratio = decay(mu[...])
    scale = -0.5 * weight[...] / root
    powers = [jnp.ones_like(ratio)]
    behind, ahead = ends[0], ends[1]
    backs = [ahead]
    for x in range(BX):
        backs.append(ratio * backs[-1])
    for x in range(XR):
        rows = slice(x * KS, (x + 1) * KS)
        value = split(scale * (local[rows, :] + behind + backs[BX - x]))
        work_high[rows, :] = value[0]
        work_low[rows, :] = value[1]
        behind = ratio * behind
    parts = []
    for part in range(2):
        columns = slice(part * HALF, (part + 1) * HALF)
        value = (work_high[:, columns], work_low[:, columns])
        parts.append(
            (
                dot3(value, (high[:HALF, columns], low[:HALF, columns]), NT),
                dot3(value, (high[HALF:, columns], low[HALF:, columns]), NT),
            )
        )
    work[:, :HALF] = parts[0][0] + parts[1][0]
    work[:, HALF:] = parts[0][0] - parts[1][0]
    extra[...] = parts[0][1] + parts[1][1]
    for t in range(4):
        for group in range(4):
            pieces = [work[x * KS : (x + 1) * KS, group * 128 : (group + 1) * 128] for x in range(4 * t, 4 * t + 4)]
            for i, piece in enumerate(exchange(pieces, 32, lane16)):
                chunk[4 * group + i, t * KS : (t + 1) * KS, :] = piece
    edges = []
    for x in range(BX):
        edges.append(
            jnp.where(lane8 < 64, extra[x * KS : x * KS + 8, :], pltpu.roll(extra[x * KS + 8 : (x + 1) * KS, :], 64, 1))
        )
    for c, piece in enumerate(exchange(edges, 1, lane8)):
        group, i = divmod(c, 4)
        for kt in range(2):
            at = BX * KS + kt * 8
            last = work[at : at + 8, group * 128 : (group + 1) * 128]
            turn = (64 * kt - 32 * i) % 128
            last = pltpu.roll(last, turn, 1) if turn else last
            piece = jnp.where(lane8 // 32 == 2 * kt, last, piece)
        chunk[c, 4 * KS :, :] = piece


def inverse(local, carries, mu, weight, high, low):
    vmem = pl.BlockSpec(memory_space=pltpu.VMEM)
    return pl.pallas_call(
        inverse_kernel,
        in_specs=[vmem] * 6,
        out_specs=vmem,
        out_shape=jax.ShapeDtypeStruct((SPAN, ROWS, 128), f32),
        scratch_shapes=[
            pltpu.VMEM((2, KS, NY), f32),
            pltpu.VMEM((XR * KS, NY), bf16),
            pltpu.VMEM((XR * KS, NY), bf16),
            pltpu.VMEM((XR * KS, NY), f32),
            pltpu.VMEM((XR * KS, 128), f32),
        ],
        name="inverse",
    )(near(local), near(carries), near(mu), near(weight), near(high), near(low))


def correct_kernel(recv, basis, es, ns, us, east, north, upward, press, buf, sems, done):
    loads = [pltpu.make_async_copy(ref, buf.at[f], sems.at[f]) for f, ref in enumerate((es, ns, us))]
    for copy in loads:
        copy.start()
    back = split(basis[...])
    for t in range(4):
        modes = split(recv[:, t * KS : (t + 1) * KS, :].reshape(NZ, 128))
        press[t * 128 : (t + 1) * 128, :] = dot3(back, modes, NN).T
    extras = []
    for s in range(SPAN):
        piece = recv[s, 4 * KS :, :]
        extras.append(piece)
        extras.append(pltpu.roll(piece, 64, 1))
    modes = split(jnp.concatenate(extras, axis=0))
    press[512:640, :] = dot3(back, modes, NN).T
    row = lax.broadcasted_iota(jnp.int32, (BY, NZ), 0)
    lane = lax.broadcasted_iota(jnp.int32, (BY, NZ), 1)

    def plane(x, here):
        beyond = press[pl.ds(pl.multiple_of((x + 1) * BY, BY), BY), :]
        edge = press[pl.ds(BX * BY + BY + x, 1), :]
        beside = jnp.where(row == BY - 1, edge, pltpu.roll(here, BY - 1, 0))
        above = jnp.where(lane == NZ - 1, 0.0, pltpu.roll(here, NZ - 1, 1))
        for f, value in enumerate((beyond, beside, above)):
            buf[f, x] = buf[f, x] - (value - here)
        return beyond

    for copy in loads:
        copy.wait()
    here = press[:BY, :]
    stores = []
    for t in range(4):
        here = lax.fori_loop(4 * t, 4 * t + 4, plane, here)
        for f, ref in enumerate((east, north, upward)):
            copy = pltpu.make_async_copy(buf.at[f, pl.ds(4 * t, 4)], ref.at[pl.ds(4 * t, 4)], done.at[t, f])
            copy.start()
            stores.append(copy)
    for copy in stores:
        copy.wait()


def correct(recv, basis, es, ns, us):
    any_spec = pl.BlockSpec(memory_space=pl.ANY)
    vmem = pl.BlockSpec(memory_space=pltpu.VMEM)
    block = jax.ShapeDtypeStruct((BX, BY, NZ), f32)
    return pl.pallas_call(
        correct_kernel,
        in_specs=[vmem] * 2 + [any_spec] * 3,
        out_specs=[any_spec] * 3,
        out_shape=[block] * 3,
        scratch_shapes=[
            pltpu.VMEM((BX * BY + 128, NZ), f32),
            pltpu.VMEM((3, BX, BY, NZ), f32),
            pltpu.SemaphoreType.DMA((3,)),
            pltpu.SemaphoreType.DMA((4, 3)),
        ],
        name="correct",
    )(near(recv), near(basis), es, ns, us)


def ring(axis, count, step, value):
    return lax.ppermute(value, axis, [(i, (i + step) % count) for i in range(count)])


def per_device(
    downflow_motion,
    crossflow_motion,
    upright_motion,
    thermal_anomaly,
    height_to_eigenbasis,
    eigenbasis_to_height,
    negated_height_spectrum,
):
    fields = (downflow_motion, crossflow_motion, upright_motion, thermal_anomaly)
    x_first, x_last, y_first, y_last = pack(fields)
    xlo = ring("aisle", AISLE, 1, x_last)
    xhi = ring("aisle", AISLE, -1, x_first)
    ylo = ring("span", SPAN, 1, y_last)
    yhi = ring("span", SPAN, -1, y_first)
    share = lax.dynamic_slice(negated_height_spectrum, (lax.axis_index("span") * KS,), (KS,))
    mu = share[:, None] + jnp.asarray(EIGEN)[None, :]
    turn = lax.axis_index("aisle")
    mu_lines = lax.dynamic_slice(mu, ((turn // 4) % 4 * 4, turn % 4 * 128), (4, 128))
    kind = (turn // 16).astype(jnp.int32).reshape(1)
    high, low = jnp.asarray(TABLE_HIGH), jnp.asarray(TABLE_LOW)
    weight = jnp.asarray(WEIGHT).reshape(1, NY)
    swap = functools.partial(lax.all_to_all, split_axis=0, concat_axis=0, tiled=True)
    es, ns, us, heat, chunk = predict(fields, xlo, xhi, ylo, yhi, height_to_eigenbasis)
    local, sums = transform(swap(chunk, "span"), mu, high, low)
    carries = carry(kind, swap(sums, "aisle"), mu_lines)
    chunk = inverse(local, swap(carries, "aisle"), mu, weight, high, low)
    east, north, upward = correct(swap(chunk, "span"), eigenbasis_to_height, es, ns, us)
    return (east, north, upward, heat)


def solution(mesh):
    block = P("aisle", "span", None)
    return jax.shard_map(
        per_device,
        mesh=mesh,
        in_specs=(block,) * 4 + (P(), P(), P()),
        out_specs=(block,) * 4,
        check_vma=False,
    )
```
